32 devices in a mesh: expert: 8 (over z, y), hidden: 4 (over x, core).
Axes of the slice: x: 2, y: 2, z: 4, core: 2. Of those that a mesh axis runs over, the one named last changes fastest.
Arguments:
- tokens: float32 [1024, 2048], P('expert', 'hidden'), may hold values from -6 to 6
- route_first: int32 [1024, 1], P('expert'), may hold values from 0 to 7; in each aligned block of 128 rows (0 to 127, 128 to 255, ...) at most 32 rows name the same one
- route_second: int32 [1024, 1], P('expert'), may hold values from 0 to 7; in each aligned block of 128 rows (0 to 127, 128 to 255, ...) at most 32 rows name the same one
- route_third: int32 [1024, 1], P('expert'), may hold values from 0 to 7; in each aligned block of 128 rows (0 to 127, 128 to 255, ...) at most 32 rows name the same one
- gate_weight: bfloat16 [8, 2048, 1024], P('expert', None, 'hidden'), may hold values from -0.125 to 0.125
- up_weight: bfloat16 [8, 2048, 1024], P('expert', None, 'hidden'), may hold values from -0.125 to 0.125
- down_weight: bfloat16 [8, 1024, 2048], P('expert', 'hidden'), may hold values from -0.1875 to 0.1875
- cotangent: float32 [1024, 2048], P('expert', 'hidden'), may hold values from -6 to 6
Outputs:
- grad_tokens: float32 [1024, 2048], P('expert', 'hidden')
- grad_gate: bfloat16 [8, 2048, 1024], P('expert', None, 'hidden')
- grad_up: bfloat16 [8, 2048, 1024], P('expert', None, 'hidden')
- grad_down: bfloat16 [8, 1024, 2048], P('expert', 'hidden')
The draws below stay inside these ranges and needn't reach their ends.
Inputs may be any that keep to these rules, and one draw needn't show every extreme that they name: `route_first`: in the rows of one index of expert, no expert is named by more than 32 tokens in one visit, a bound that some block reaches; every expert is named somewhere. `route_second`: as for route_first. `route_third`: as for route_first.
All inputs are finite; a program needn't handle non-finite values.
Results may differ from the reference program's by a relative error of at most 0.024.
Values may be sent and summed in bfloat16 or wider, within the bound.
No kernel may reach another device: no remote copies, remote signals or barrier semaphores. Data moves between devices by JAX's collectives and lax.ppermute only.
A program may use at most 64 MiB of HBM per device.

```python
import math
import jax
import jax.numpy as jnp
import numpy as np
from jax import lax

D = 2048
FF = 1024
TOK_DEV = 128
EXPERTS = 8
TOKENS = 1024
CAP = 32
EXPERT_ROWS = 256
N_EXPERT = 8


def steps_of(rng, shape, shards, least, high):
    factor_of, own = 1.0, jax.random.fold_in(rng, 6)
    for position, parts in shards:
        steps = jnp.exp(jax.random.uniform(jax.random.fold_in(own, position), (parts,), jnp.float32, least / len(shards), high / len(shards)))
        factor_of = factor_of * jnp.repeat(steps, shape[position] // parts).reshape([-1 if axis == position else 1 for axis in range(len(shape))])
    return factor_of


def deal_out(own_key, own, number, rows, count, top, most, lean):
    sequence = jax.random.permutation(own_key, count)
    crowded, common = load_shares(count, rows * top, most, lean, True), load_shares(count, rows * top, most, lean, False)
    places = jnp.arange(count)

    def named(sizes, rotation):
        used = int((sizes > 0).sum())
        fixed = max(1, used // 4)
        shifted = fixed + (places - fixed + rotation * (used - fixed)) % max(1, count - fixed)
        return jnp.zeros((count,), jnp.int32).at[sequence[jnp.where(places < fixed, places, shifted)]].set(jnp.asarray(sizes, jnp.int32))

    sizes = jnp.where(number % 4 == 0, named(crowded, number // 4), named(common, number - number // 4 - 1))
    mixed = jax.random.permutation(jax.random.fold_in(own, 3), count)
    giver, sink = mixed[0:count // 2 * 2:2], mixed[1:count // 2 * 2:2]
    margin = jnp.minimum(sizes[giver] - 1, most - sizes[sink]) // 2
    margin = jnp.where((giver == sequence[0]) | (sink == sequence[0]) | (sizes[sink] == 0), 0, jnp.maximum(margin, 0))
    shifted = jax.random.randint(jax.random.fold_in(own, 4), (count // 2,), 0, 1 << 20) % (margin + 1)
    sizes = sizes.at[giver].add(-shifted).at[sink].add(shifted)
    labels = jnp.searchsorted(jnp.cumsum(sizes), jnp.arange(rows * top), side="right").astype(jnp.int32)
    grid = labels.reshape(top, rows).T
    grid = grid[jax.random.permutation(jax.random.fold_in(own, 1), rows)]
    rotation = jax.random.randint(jax.random.fold_in(own, 2), (rows, 1), 0, top)
    return jnp.take_along_axis(grid, (jnp.arange(top)[None, :] + rotation) % top, axis=1)


def load_shares(count, total, limit, lean, full):
    portions = [(1 << 20) // math.isqrt(grade ** lean) + 1 for grade in range(1, count + 1)]
    largest = limit if full else min(limit, max(-(-total // count), total * portions[0] // sum(portions)))
    least = 1 if total - largest >= count - 1 else 0
    holding, rest = [largest] + [least] * (count - 1), total - largest - least * (count - 1)
    while rest > 0:
        candidates = [i for i in range(1, count) if holding[i] < largest] or [i for i in range(1, count) if holding[i] < limit]
        pool, budget = sum([portions[i] for i in candidates]), rest
        for i in candidates:
            extra = min(limit - holding[i], max(1, budget * portions[i] // pool), rest)
            holding[i] = holding[i] + extra
            rest = rest - extra
    return np.array(holding)


def scatter_about(stream_key, dims, deviation, reach, cuts=(), kind=jnp.bfloat16):
    entries = jax.random.normal(stream_key, dims, jnp.float32) * deviation
    if len(cuts) > 0:
        entries = steps_of(stream_key, dims, cuts, -0.22, 0.18) * entries
    return jnp.clip(entries, min=-reach, max=reach).astype(kind)


def setup_inputs(seed: int = 0) -> dict:
    streams_of = jax.random.split(jax.random.key(seed), 9)
    tokens = scatter_about(streams_of[0], (TOKENS, D), 1.0, 6.0, ((0, 8), (1, 4)), jnp.float32)
    route_first_keys = jax.random.split(jax.random.fold_in(streams_of[1], 1), TOKENS // TOK_DEV)
    route_first_turns = jax.random.permutation(jax.random.fold_in(streams_of[1], 3), TOKENS // TOK_DEV)
    route_first = jax.vmap(lambda own, number: deal_out(jax.random.fold_in(streams_of[1], 2), own, number, TOK_DEV, EXPERTS, 1, CAP, 2))(route_first_keys, route_first_turns).reshape((TOKENS, 1))
    route_second_keys = jax.random.split(jax.random.fold_in(streams_of[2], 1), TOKENS // TOK_DEV)
    route_second_turns = jax.random.permutation(jax.random.fold_in(streams_of[2], 3), TOKENS // TOK_DEV)
    route_second = jax.vmap(lambda own, number: deal_out(jax.random.fold_in(streams_of[2], 2), own, number, TOK_DEV, EXPERTS, 1, CAP, 2))(route_second_keys, route_second_turns).reshape((TOKENS, 1))
    route_third_keys = jax.random.split(jax.random.fold_in(streams_of[3], 1), TOKENS // TOK_DEV)
    route_third_turns = jax.random.permutation(jax.random.fold_in(streams_of[3], 3), TOKENS // TOK_DEV)
    route_third = jax.vmap(lambda own, number: deal_out(jax.random.fold_in(streams_of[3], 2), own, number, TOK_DEV, EXPERTS, 1, CAP, 2))(route_third_keys, route_third_turns).reshape((TOKENS, 1))
    gate_weight = scatter_about(streams_of[4], (EXPERTS, D, FF), D ** -0.5, 0.125, ((0, 8), (2, 4)))
    up_weight = scatter_about(streams_of[5], (EXPERTS, D, FF), D ** -0.5, 0.125, ((0, 8), (2, 4)))
    down_weight = scatter_about(streams_of[6], (EXPERTS, FF, D), FF ** -0.5, 0.1875, ((0, 8), (1, 4)))
    cotangent = scatter_about(streams_of[7], (TOKENS, D), 1.0, 6.0, ((0, 8), (1, 4)), jnp.float32)
    return {"tokens": tokens, "route_first": route_first, "route_second": route_second, "route_third": route_third, "gate_weight": gate_weight, "up_weight": up_weight, "down_weight": down_weight, "cotangent": cotangent}


def slot_index(route):
    owner_ids = route[:, 0].astype(jnp.int32)
    onehot = (owner_ids[:, None] == jnp.arange(EXPERTS, dtype=jnp.int32)[None, :]).astype(jnp.int32)
    blocks = onehot.reshape(N_EXPERT, TOK_DEV, EXPERTS)
    before = jnp.cumsum(blocks, axis=1) - blocks
    ranks = jnp.sum(before * blocks, axis=2).reshape(-1)
    source = jnp.arange(TOKENS, dtype=jnp.int32) // TOK_DEV
    return (owner_ids * EXPERT_ROWS + source * CAP + ranks).astype(jnp.int32)


def dispatch(rows, slots):
    table = jnp.zeros((EXPERTS * EXPERT_ROWS, D), rows.dtype).at[slots].set(rows)
    return table.reshape(EXPERTS, EXPERT_ROWS, D)


def combine(table, slots):
    return table.reshape(EXPERTS * EXPERT_ROWS, D)[slots]


def front(packed):
    inputs, gate_w, lift_w = packed
    return (jnp.dot(inputs, gate_w, preferred_element_type=jnp.float32),
            jnp.dot(inputs, lift_w, preferred_element_type=jnp.float32))


def project(packed):
    hidden, down_w = packed
    return jnp.dot(hidden, down_w, preferred_element_type=jnp.float32)


def backward_expert(packed):
    inputs, gate, lifted, grad_rows, gate_w, lift_w, down_w = packed
    sigma = jax.nn.sigmoid(gate)
    swish = gate * sigma
    hidden = (swish * lifted).astype(jnp.bfloat16)
    grad_down = jnp.dot(hidden.T, grad_rows, preferred_element_type=jnp.float32)
    grad_hidden = jnp.dot(grad_rows, down_w.T, preferred_element_type=jnp.float32)
    grad_gate = (grad_hidden * lifted * sigma * (1.0 + gate * (1.0 - sigma))).astype(jnp.bfloat16)
    grad_lift = (grad_hidden * swish).astype(jnp.bfloat16)
    weight_gate = jnp.dot(inputs.T, grad_gate, preferred_element_type=jnp.float32)
    weight_lift = jnp.dot(inputs.T, grad_lift, preferred_element_type=jnp.float32)
    grad_inputs = (jnp.dot(grad_gate, gate_w.T, preferred_element_type=jnp.float32)
                   + jnp.dot(grad_lift, lift_w.T, preferred_element_type=jnp.float32))
    return weight_gate, weight_lift, grad_down, grad_inputs


def reference(tokens, route_first, route_second, route_third, gate_weight, up_weight, down_weight, cotangent):
    slot_list = [slot_index(route_first), slot_index(route_second), slot_index(route_third)]
    state = tokens
    saved = []
    for visit in range(3):
        slots = slot_list[visit]
        inputs = dispatch(state.astype(jnp.bfloat16), slots)
        gate, lifted = lax.map(front, (inputs, gate_weight, up_weight))
        saved.append((inputs, gate, lifted))
        if visit < 2:
            hidden = (jax.nn.sigmoid(gate) * gate * lifted).astype(jnp.bfloat16)
            outputs = lax.map(project, (hidden, down_weight))
            state = state + combine(outputs, slots)
    grad = cotangent
    total_gate = jnp.zeros((EXPERTS, D, FF), jnp.float32)
    total_lift = jnp.zeros((EXPERTS, D, FF), jnp.float32)
    total_down = jnp.zeros((EXPERTS, FF, D), jnp.float32)
    for visit in (2, 1, 0):
        slots = slot_list[visit]
        inputs, gate, lifted = saved[visit]
        grad_rows = dispatch(grad.astype(jnp.bfloat16), slots)
        weight_gate, weight_lift, grad_down, grad_inputs = lax.map(
            backward_expert, (inputs, gate, lifted, grad_rows, gate_weight, up_weight, down_weight))
        total_gate = total_gate + weight_gate
        total_lift = total_lift + weight_lift
        total_down = total_down + grad_down
        grad = grad + combine(grad_inputs, slots)
    return (grad, total_gate.astype(jnp.bfloat16), total_lift.astype(jnp.bfloat16),
            total_down.astype(jnp.bfloat16))
```

```python
import jax
import jax.numpy as jnp
from jax import lax
from jax.sharding import PartitionSpec as P

BF16 = jnp.bfloat16
F32 = jnp.float32


def slot_table(route, experts, capacity):
    owner_ids = route[:, 0]
    onehot = (owner_ids[:, None] == jnp.arange(experts, dtype=jnp.int32)[None, :]).astype(jnp.int32)
    ranks = jnp.sum((jnp.cumsum(onehot, axis=0) - onehot) * onehot, axis=1)
    slots = owner_ids * capacity + ranks
    total = experts * capacity
    table = slots[None, :] == jnp.arange(total, dtype=jnp.int32)[:, None]
    return table.astype(BF16)


def contract_first(left, right):
    return lax.dot_general(left, right, (((0,), (0,)), ((), ())), preferred_element_type=F32)


def contract_last(left, right):
    return lax.dot_general(left, right, (((1,), (1,)), ((), ())), preferred_element_type=F32)


def dot(left, right):
    return jnp.dot(left, right, preferred_element_type=F32)


def swap(value, bit, group):
    return lax.ppermute(value, "hidden", [(i, i ^ bit) for i in range(group)])


def over_experts(rows, experts):
    width = rows.shape[1]
    moved = lax.all_to_all(
        rows.reshape(experts, -1, width), "expert", split_axis=0, concat_axis=0, tiled=True
    )
    return moved.reshape(-1, width)


def gather_hidden(rows, group):
    bit = group // 2
    have = {0: rows}
    while bit >= 1:
        for j in list(have):
            have[j ^ bit] = swap(have[j], bit, group)
        bit //= 2
    return [have[j] for j in range(group)]


def scatter_hidden(partial_of, group):
    def total(j, bits):
        if not bits:
            return partial_of(j)
        rest, last = bits[:-1], bits[-1]
        away = total(j ^ last, rest)
        here = total(j, rest)
        return here + swap(away.astype(BF16), last, group).astype(F32)

    bits = []
    while 1 << len(bits) < group:
        bits.append(1 << len(bits))
    return total(0, bits)


def body(
    tokens, route_first, route_second, route_third, gate_weight, up_weight, down_weight, cotangent
):
    experts = lax.axis_size("expert")
    group = lax.axis_size("hidden")
    me = lax.axis_index("hidden")
    count, chunk = tokens.shape
    capacity = 2 * count // experts
    width = gate_weight.shape[2]
    both = jnp.concatenate([gate_weight[0], up_weight[0]], axis=1)
    down = down_weight[0]
    both_of = [lax.dynamic_slice_in_dim(both, (me ^ j) * chunk, chunk, 0) for j in range(group)]
    down_of = [lax.dynamic_slice_in_dim(down, (me ^ j) * chunk, chunk, 1) for j in range(group)]
    tables = [
        slot_table(route, experts, capacity) for route in (route_first, route_second, route_third)
    ]

    def dispatch(values, table):
        placed = dot(table, values.astype(BF16)).astype(BF16)
        return gather_hidden(over_experts(placed, experts), group)

    def home(partial_of, table):
        shared = scatter_hidden(partial_of, group).astype(BF16)
        return contract_first(table, over_experts(shared, experts))

    state = tokens
    saved = []
    last_rows = dispatch(cotangent, tables[2])
    for visit in range(3):
        inputs = dispatch(state, tables[visit])
        pre = dot(inputs[0], both_of[0])
        for j in range(1, group):
            pre = pre + dot(inputs[j], both_of[j])
        gate, lifted = pre[:, :width], pre[:, width:]
        sigma = jax.nn.sigmoid(gate)
        swish = gate * sigma
        hidden = (swish * lifted).astype(BF16)
        saved.append((inputs, gate, lifted, hidden))
        if visit < 2:
            state = state + home(lambda j: dot(hidden, down_of[j]), tables[visit])
    grad = cotangent
    rows_list = [None] * 3
    both_list = [None] * 3
    for visit in (2, 1, 0):
        inputs, gate, lifted, hidden = saved[visit]
        grad_rows = last_rows if visit == 2 else dispatch(grad, tables[visit])
        sigma = jax.nn.sigmoid(gate)
        swish = gate * sigma
        grad_hidden = contract_last(grad_rows[0], down_of[0])
        for j in range(1, group):
            grad_hidden = grad_hidden + contract_last(grad_rows[j], down_of[j])
        grad_gate = (grad_hidden * lifted * sigma * (1.0 + gate * (1.0 - sigma))).astype(BF16)
        grad_lift = (grad_hidden * swish).astype(BF16)
        grad_both = jnp.concatenate([grad_gate, grad_lift], axis=1)
        rows_list[visit] = grad_rows
        both_list[visit] = grad_both
        grad = grad + home(lambda j: contract_last(grad_both, both_of[j]), tables[visit])

    hidden_all = jnp.concatenate([saved[v][3] for v in range(3)], axis=0)
    both_all = jnp.concatenate(both_list, axis=0)
    out_gate = jnp.zeros(gate_weight.shape[1:], BF16)
    out_up = jnp.zeros(up_weight.shape[1:], BF16)
    out_down = jnp.zeros(down_weight.shape[1:], BF16)
    for j in range(group):
        inputs_all = jnp.concatenate([saved[v][0][j] for v in range(3)], axis=0)
        rows_all = jnp.concatenate([rows_list[v][j] for v in range(3)], axis=0)
        place = (me ^ j) * chunk
        total = contract_first(inputs_all, both_all).astype(BF16)
        out_gate = lax.dynamic_update_slice_in_dim(out_gate, total[:, :width], place, 0)
        out_up = lax.dynamic_update_slice_in_dim(out_up, total[:, width:], place, 0)
        total = contract_first(hidden_all, rows_all).astype(BF16)
        out_down = lax.dynamic_update_slice_in_dim(out_down, total, place, 1)
    return grad, out_gate[None], out_up[None], out_down[None]


def solution(mesh):
    placed = (
        P("expert", "hidden"),
        P("expert", None),
        P("expert", None),
        P("expert", None),
        P("expert", None, "hidden"),
        P("expert", None, "hidden"),
        P("expert", "hidden", None),
        P("expert", "hidden"),
    )
    return jax.shard_map(
        body,
        mesh=mesh,
        in_specs=placed,
        out_specs=(
            P("expert", "hidden"),
            P("expert", None, "hidden"),
            P("expert", None, "hidden"),
            P("expert", "hidden", None),
        ),
        check_vma=False,
    )
```

```python
import functools

import jax
import jax.numpy as jnp
from jax import lax
from jax.experimental import pallas as pl
from jax.experimental.pallas import tpu as pltpu
from jax.sharding import Mesh, PartitionSpec as P


BF16 = jnp.bfloat16
F32 = jnp.float32
SMALL = pltpu.CompilerParams(vmem_limit_bytes=32 << 20)


def contract_first(left, right):
    return lax.dot_general(left, right, (((0,), (0,)), ((), ())), preferred_element_type=F32)


def contract_last(left, right):
    return lax.dot_general(left, right, (((1,), (1,)), ((), ())), preferred_element_type=F32)


def dot(left, right):
    return jnp.dot(left, right, preferred_element_type=F32)


def add(terms):
    total = terms[0]
    for term in terms[1:]:
        total = total + term
    return total


def after(value, *others):
    return lax.optimization_barrier((value,) + others)[0]


def slot_rows(route, experts, capacity):
    count = route.shape[1]
    onehot = route == lax.broadcasted_iota(jnp.int32, (experts, count), 0)
    earlier = lax.broadcasted_iota(jnp.int32, (count, count), 0) < lax.broadcasted_iota(
        jnp.int32, (count, count), 1
    )
    before = dot(onehot.astype(F32).astype(BF16), earlier.astype(F32).astype(BF16))
    rank = jnp.sum(jnp.where(onehot, before, 0.0), axis=0, keepdims=True).astype(jnp.int32)
    slot = route * capacity + rank
    total = experts * capacity
    return (slot == lax.broadcasted_iota(jnp.int32, (total, count), 0)).astype(F32).astype(BF16)


def start_kernel(experts, capacity, route_hbm, values_hbm, table_ref, placed_ref, *scratch):
    route_ref, values_ref, route_sem, values_sem = scratch
    route_load = pltpu.make_async_copy(route_hbm, route_ref, route_sem)
    values_load = pltpu.make_async_copy(values_hbm, values_ref, values_sem)
    route_load.start()
    values_load.start()
    route_load.wait()
    table = slot_rows(route_ref[...], experts, capacity)
    table_ref[...] = table
    values_load.wait()
    placed_ref[...] = dot(table, values_ref[...].astype(BF16)).astype(BF16)


def start(route, values, experts, capacity):
    count, chunk = values.shape
    total = experts * capacity
    return pl.pallas_call(
        functools.partial(start_kernel, experts, capacity),
        in_specs=[pl.BlockSpec(memory_space=pl.ANY)] * 2,
        out_shape=(
            jax.ShapeDtypeStruct((total, count), BF16),
            jax.ShapeDtypeStruct((total, chunk), BF16),
        ),
        scratch_shapes=[
            pltpu.VMEM((1, count), jnp.int32),
            pltpu.VMEM((count, chunk), F32),
            pltpu.SemaphoreType.DMA,
            pltpu.SemaphoreType.DMA,
        ],
        cost_estimate=pl.CostEstimate(
            flops=2 * total * count * chunk, bytes_accessed=1 << 20, transcendentals=0
        ),
        name="start",
    )(route.reshape(1, count), values)


def table_kernel(experts, capacity, route_ref, table_ref):
    table_ref[...] = slot_rows(route_ref[...], experts, capacity)


def turn_kernel(from_ref, to_ref, moved_ref, state_ref, state_out_ref, placed_ref):
    slots = from_ref.shape[0]
    state = state_ref[...]
    for begin in range(0, moved_ref.shape[0], slots):
        state = state + contract_first(from_ref[...], moved_ref[begin : begin + slots, :])
    state_out_ref[...] = state
    placed_ref[...] = dot(to_ref[...], state.astype(BF16)).astype(BF16)


def turn(table_from, table_to, moved, state):
    return pl.pallas_call(
        turn_kernel,
        out_shape=(
            jax.ShapeDtypeStruct(state.shape, F32),
            jax.ShapeDtypeStruct((table_to.shape[0], state.shape[1]), BF16),
        ),
        compiler_params=SMALL,
        cost_estimate=pl.CostEstimate(
            flops=4 * moved.shape[0] * state.size, bytes_accessed=1 << 20, transcendentals=0
        ),
        name="turn",
    )(table_from, table_to, moved, state)


def front_grads_kernel(visits, group, spots_ref, *refs):
    rights, lefts = refs[:visits], refs[visits : visits * (1 + group)]
    gate_ref, up_ref, left_buf, out_buf, in_sem, out_sem = refs[visits * (1 + group) :]
    chunk, width = left_buf.shape[3], gate_ref.shape[1]
    loads = []
    for j in range(group):
        for v in range(visits):
            load = pltpu.make_async_copy(
                lefts[v * group + j], left_buf.at[j, v], in_sem.at[j, v]
            )
            load.start()
            loads.append(load)
    stores = []
    for j in range(group):
        total = None
        for v in range(visits):
            loads[j * visits + v].wait()
            term = contract_first(left_buf[j, v], rights[v][...])
            total = term if total is None else total + term
        out_buf[j, 0] = total[:, :width].astype(BF16)
        out_buf[j, 1] = total[:, width:].astype(BF16)
        spot = pl.multiple_of(spots_ref[j], chunk)
        for side, ref in enumerate((gate_ref, up_ref)):
            store = pltpu.make_async_copy(
                out_buf.at[j, side], ref.at[pl.ds(spot, chunk)], out_sem.at[j, side]
            )
            store.start()
            stores.append(store)
    for store in stores:
        store.wait()


def front_grads(spots, grads):
    visits, group = len(grads), len(grads[0][1])
    rows, chunk = grads[0][1][0].shape
    width = grads[0][0].shape[1] // 2
    out = jax.ShapeDtypeStruct((group * chunk, width), BF16)
    return pl.pallas_call(
        functools.partial(front_grads_kernel, visits, group),
        in_specs=[pl.BlockSpec(memory_space=pltpu.SMEM)]
        + [pl.BlockSpec(memory_space=pltpu.VMEM)] * visits
        + [pl.BlockSpec(memory_space=pl.ANY)] * (visits * group),
        out_specs=(pl.BlockSpec(memory_space=pl.ANY),) * 2,
        out_shape=(out, out),
        scratch_shapes=[
            pltpu.VMEM((group, visits, rows, chunk), BF16),
            pltpu.VMEM((group, 2, chunk, width), BF16),
            pltpu.SemaphoreType.DMA((group, visits)),
            pltpu.SemaphoreType.DMA((group, 2)),
        ],
        cost_estimate=pl.CostEstimate(
            flops=4 * visits * rows * group * chunk * width,
            bytes_accessed=2 * visits * rows * group * chunk + 4 * group * chunk * width,
            transcendentals=0,
        ),
        name="front_grads",
    )(spots, *[right for right, _ in grads], *[left for _, lefts in grads for left in lefts])


def down_grads_kernel(visits, group, spots_ref, *refs):
    lefts, rights = refs[:visits], refs[visits : visits * (1 + group)]
    out_ref, right_buf, out_buf, in_sem, out_sem = refs[visits * (1 + group) :]
    chunk = right_buf.shape[3]
    loads = []
    for j in range(group):
        for v in range(visits):
            load = pltpu.make_async_copy(
                rights[v * group + j], right_buf.at[j, v], in_sem.at[j, v]
            )
            load.start()
            loads.append(load)
    stores = []
    for j in range(group):
        total = None
        for v in range(visits):
            loads[j * visits + v].wait()
            term = contract_first(lefts[v][...], right_buf[j, v])
            total = term if total is None else total + term
        out_buf[j] = total.astype(BF16)
        spot = pl.multiple_of(spots_ref[j], chunk)
        store = pltpu.make_async_copy(
            out_buf.at[j], out_ref.at[:, pl.ds(spot, chunk)], out_sem.at[j]
        )
        store.start()
        stores.append(store)
    for store in stores:
        store.wait()


def down_grads(spots, lowers):
    visits, group = len(lowers), len(lowers[0][1])
    rows, chunk = lowers[0][1][0].shape
    width = lowers[0][0].shape[1]
    return pl.pallas_call(
        functools.partial(down_grads_kernel, visits, group),
        in_specs=[pl.BlockSpec(memory_space=pltpu.SMEM)]
        + [pl.BlockSpec(memory_space=pltpu.VMEM)] * visits
        + [pl.BlockSpec(memory_space=pl.ANY)] * (visits * group),
        out_specs=pl.BlockSpec(memory_space=pl.ANY),
        out_shape=jax.ShapeDtypeStruct((width, group * chunk), BF16),
        scratch_shapes=[
            pltpu.VMEM((group, visits, rows, chunk), BF16),
            pltpu.VMEM((group, width, chunk), BF16),
            pltpu.SemaphoreType.DMA((group, visits)),
            pltpu.SemaphoreType.DMA((group,)),
        ],
        cost_estimate=pl.CostEstimate(
            flops=2 * visits * rows * group * chunk * width,
            bytes_accessed=2 * visits * rows * group * chunk + 2 * group * chunk * width,
            transcendentals=0,
        ),
        name="down_grads",
    )(spots, *[left for left, _ in lowers], *[right for _, rights in lowers for right in rights])


def combine_kernel(halves, parts, last, left_ref, *refs):
    weights, received, out_ref = refs[:halves], refs[halves:-1], refs[-1]
    rows = left_ref.shape[0]
    for x in range(halves):
        if last:
            total = contract_last(left_ref[...], weights[x][...])
        else:
            total = dot(left_ref[...], weights[x][...])
        for k in range(parts - 1):
            total = total + received[x * (parts - 1) + k][...].astype(F32)
        out_ref[pl.ds(x * rows, rows), :] = total.astype(BF16)


def combine(left, weights, received, last):
    halves, rows = len(weights), left.shape[0]
    chunk = weights[0].shape[0 if last else 1]
    return pl.pallas_call(
        functools.partial(combine_kernel, halves, len(received) // halves + 1, last),
        out_shape=jax.ShapeDtypeStruct((halves * rows, chunk), BF16),
        compiler_params=SMALL,
        cost_estimate=pl.CostEstimate(
            flops=2 * halves * rows * left.shape[1] * chunk,
            bytes_accessed=2 << 20,
            transcendentals=0,
        ),
        name="combine",
    )(left, *weights, *received)


def silu_terms(pre):
    width = pre.shape[1] // 2
    gate, lifted = pre[:, :width], pre[:, width:]
    sigma = jax.nn.sigmoid(gate)
    return gate, lifted, sigma, gate * sigma


def late_kernel(forward, backward, acc_ref, rows_ref, weight_ref, *refs):
    refs = list(refs)
    other_ref = refs.pop(0) if backward else None
    outs = (2 if forward and not backward else 1) + (1 if forward and backward else 0)
    away = (len(refs) - outs) // 2
    weights, refs = refs[:away], refs[away:]
    if forward:
        pre = acc_ref[...] + dot(rows_ref[...], weight_ref[...])
    else:
        pre = other_ref[...]
    gate, lifted, sigma, swish = silu_terms(pre)
    if forward:
        hidden = (swish * lifted).astype(BF16)
        refs.pop(0)[...] = hidden
    if not backward:
        refs.pop(0)[...] = pre
        for weight, out_ref in zip(weights, refs):
            out_ref[...] = dot(hidden, weight[...]).astype(BF16)
        return
    if forward:
        pull = other_ref[...]
    else:
        pull = acc_ref[...] + contract_last(rows_ref[...], weight_ref[...])
    width = lifted.shape[1]
    both_ref = refs.pop(0)
    both_ref[:, :width] = (pull * lifted * sigma * (1.0 + gate * (1.0 - sigma))).astype(BF16)
    both_ref[:, width:] = (pull * swish).astype(BF16)
    for weight, out_ref in zip(weights, refs):
        out_ref[...] = contract_last(both_ref[...], weight[...]).astype(BF16)


def late(acc, rows, weight, away, other=None, forward=True):
    count, chunk = rows.shape
    backward = other is not None
    width = (acc.shape[1] if forward else acc.shape[1] * 2) // 2
    out = []
    if forward:
        out.append(jax.ShapeDtypeStruct((count, width), BF16))
    if not backward:
        out.append(jax.ShapeDtypeStruct((count, 2 * width), F32))
    else:
        out.append(jax.ShapeDtypeStruct((count, 2 * width), BF16))
    out += [jax.ShapeDtypeStruct((count, chunk), BF16)] * len(away)
    args = (acc, rows, weight) + ((other,) if backward else ()) + tuple(away)
    return pl.pallas_call(
        functools.partial(late_kernel, forward, backward),
        out_shape=tuple(out),
        compiler_params=SMALL,
        cost_estimate=pl.CostEstimate(
            flops=4 * count * chunk * width * (1 + len(away)),
            bytes_accessed=4 << 20,
            transcendentals=count * width,
        ),
        name="late",
    )(*args)


def body(
    tokens, route_first, route_second, route_third, gate_weight, up_weight, down_weight, cotangent
):
    experts = lax.axis_size("expert")
    halves = lax.axis_size("row")
    parts = lax.axis_size("part")
    row = lax.axis_index("row")
    part = lax.axis_index("part")
    count, chunk = tokens.shape
    capacity = 2 * count // experts
    both = jnp.concatenate([gate_weight[0], up_weight[0]], axis=1)
    down = down_weight[0]

    def chunk_of(x, k):
        return (x * parts + (part ^ k)) * chunk

    near = [(i, k) for i in range(halves) for k in range(parts)]
    spots = [chunk_of(row ^ i, k) for i, k in near]
    both_near = [lax.dynamic_slice_in_dim(both, spot, chunk, 0) for spot in spots]
    down_near = [lax.dynamic_slice_in_dim(down, spot, chunk, 1) for spot in spots]
    both_at = {ik: lax.dynamic_slice_in_dim(both, chunk_of(*ik), chunk, 0) for ik in near}
    down_at = {ik: lax.dynamic_slice_in_dim(down, chunk_of(*ik), chunk, 1) for ik in near}

    def swap(value, axis, step):
        size = lax.axis_size(axis)
        return lax.ppermute(value, axis, [(i, i ^ step) for i in range(size)])

    def over_experts(rows):
        moved = lax.all_to_all(
            rows.reshape(experts, capacity, chunk), "expert", split_axis=0, concat_axis=0, tiled=True
        )
        return moved.reshape(experts * capacity, chunk)

    def gather(rows):
        have = {(0, 0): rows}
        for i in range(1, halves):
            have[i, 0] = swap(rows, "row", i)
        for i in range(halves):
            for k in range(1, parts):
                have[i, k] = swap(have[i, 0], "part", k)
        return [have[ik] for ik in near]

    far = [(x, k) for x in range(halves) for k in range(1, parts)]

    def reduce_parts(left, away, weights, last):
        received = [swap(value, "part", k) for (_, k), value in zip(far, away)]
        return combine(left, [weights[x, 0] for x in range(halves)], received, last)

    def send_home(shared):
        moved = lax.all_to_all(
            shared.reshape(halves * experts, capacity, chunk),
            ("row", "expert"),
            split_axis=0,
            concat_axis=0,
            tiled=True,
        )
        return moved.reshape(halves * experts * capacity, chunk)

    table_first, placed = start(route_first, tokens, experts, capacity)
    table_third, cot_placed = start(route_third, cotangent, experts, capacity)
    table_second = pl.pallas_call(
        functools.partial(table_kernel, experts, capacity),
        out_shape=jax.ShapeDtypeStruct(table_first.shape, BF16),
        compiler_params=SMALL,
        name="table",
    )(route_second.reshape(1, count))
    tables = [table_first, table_second, table_third]

    def pull_back(grad_rows):
        return add([contract_last(rows, low) for rows, low in zip(grad_rows, down_near)])

    def front(inputs):
        return add([dot(rows, weight) for rows, weight in zip(inputs, both_near)])

    down_away = [down_at[ik] for ik in far]
    both_away = [both_at[ik] for ik in far]
    state = tokens
    inputs_of, pre_of, hidden_of = [], [], []
    for visit in range(3):
        arrived = over_experts(placed)
        if visit == 0:
            arrived = after(arrived, cot_placed, table_second, *both_near[1:], *down_away)
        if visit == 2:
            pull = pull_back(last_rows)
            arrived = after(arrived, pull)
        inputs = gather(arrived)
        inputs_of.append(inputs)
        if visit == 0:
            cot_arrived = over_experts(cot_placed)
        if visit == 1:
            last_rows = gather(cot_arrived)
        if visit < 2:
            hidden, pre, *away = late(front(inputs[:-1]), inputs[-1], both_near[-1], down_away)
            pre_of.append(pre)
            hidden_of.append(hidden)
            shared = reduce_parts(hidden, away, down_at, False)
            if visit == 0:
                shared = after(shared, cot_arrived)
            state, placed = turn(tables[visit], tables[visit + 1], send_home(shared), state)

    grad = cotangent
    grads, lowers = [], []
    for visit in (2, 1, 0):
        inputs = inputs_of[visit]
        if visit == 2:
            grad_rows = last_rows
            hidden, grad_both, *away = late(
                front(inputs[:-1]), inputs[-1], both_near[-1], both_away, pull
            )
            hidden_of.append(hidden)
        else:
            grad_rows = gather(over_experts(placed))
            grad_both, *away = late(
                pull_back(grad_rows[:-1]),
                grad_rows[-1],
                down_near[-1],
                both_away,
                pre_of[visit],
                forward=False,
            )
        shared = reduce_parts(grad_both, away, both_at, True)
        moved = send_home(shared)
        if visit > 0:
            grad, placed = turn(tables[visit], tables[visit - 1], moved, grad)
        else:
            grad = add(
                [grad] + [contract_first(tables[visit], term) for term in jnp.split(moved, halves)]
            )
            grad_both = after(grad_both, shared)
        grads.append((grad_both, inputs))
        lowers.append((hidden_of[visit], grad_rows))

    spots = jnp.stack(spots).astype(jnp.int32)
    out_down = down_grads(spots, lowers)
    out_gate, out_up = front_grads(spots, grads)
    return grad, out_gate[None], out_up[None], out_down[None]


def solution(mesh):
    experts, group = mesh.shape["expert"], mesh.shape["hidden"]
    halves = 2 if group % 2 == 0 else 1
    hidden = ("row", "part")
    fine = Mesh(mesh.devices.reshape(experts, halves, group // halves), ("expert",) + hidden)
    placed = (
        P("expert", hidden),
        P("expert", None),
        P("expert", None),
        P("expert", None),
        P("expert", None, hidden),
        P("expert", None, hidden),
        P("expert", hidden, None),
        P("expert", hidden),
    )

    return jax.shard_map(
        body,
        mesh=fine,
        in_specs=placed,
        out_specs=(
            P("expert", hidden),
            P("expert", None, hidden),
            P("expert", None, hidden),
            P("expert", hidden, None),
        ),
        check_vma=False,
    )
```
